32 devices in a mesh: dp: 4 (over z), ctx: 2 (over x), tensor: 4 (over y, core).
Axes of the slice: x: 2, y: 2, z: 4, core: 2. Of those that a mesh axis runs over, the one named last changes fastest.
Arguments:
- tokens: bfloat16 [2048, 8, 512], P(('ctx', 'tensor'), 'dp'), may hold values from -6 to 6
- segments: int32 [8, 2048], P('dp'), may hold values from 0 to 7, never falling along the last dimension, each value on 1 to 1024 neighbouring positions
- scales: float32 [512], replicated, may hold values from 0.1 to 1.9
- shifts: float32 [512], replicated, may hold values from -3 to 3
- project: bfloat16 [512, 3, 512], P(None, None, 'tensor'), may hold values from -0.25 to 0.25
- combine: bfloat16 [512, 512], P('tensor'), may hold values from -0.75 to 0.75
- stretch: float32 [512], replicated, may hold values from 0.1 to 1.9
- offset: float32 [512], replicated, may hold values from -3 to 3
- expand: bfloat16 [512, 2048], P(None, 'tensor'), may hold values from -0.25 to 0.25
- boosts: float32 [2048], P('tensor'), may hold values from -3 to 3
- shrink: bfloat16 [2048, 512], P('tensor'), may hold values from -0.125 to 0.125
- biases: float32 [512], replicated, may hold values from -3 to 3
- cotangent: bfloat16 [2048, 8, 512], P(('ctx', 'tensor'), 'dp'), may hold values from -6 to 6
Outputs:
- encoded: bfloat16 [2048, 8, 512], P(('ctx', 'tensor'), 'dp')
- delta_tokens: float32 [2048, 8, 512], P(('ctx', 'tensor'), 'dp')
- delta_scales: float32 [512], replicated
- delta_shifts: float32 [512], replicated
- delta_project: float32 [512, 3, 512], P(None, None, 'tensor')
- delta_combine: float32 [512, 512], P('tensor')
- delta_stretch: float32 [512], replicated
- delta_offset: float32 [512], replicated
- delta_expand: float32 [512, 2048], P(None, 'tensor')
- delta_boosts: float32 [2048], P('tensor')
- delta_shrink: float32 [2048, 512], P('tensor')
- delta_biases: float32 [512], replicated
The draws below stay inside these ranges and needn't reach their ends.
Inputs may be any that keep to these rules, and one draw needn't show every extreme that they name: `segments`: along each sequence the document numbers never fall, every number between the least and the greatest occurs, and the longest document has exactly 1024 positions.
All inputs are finite; a program needn't handle non-finite values.
Results may differ from the reference program's by a relative error of at most 0.02.
Values may be sent and summed in bfloat16 or wider, within the bound.
No kernel may reach another device: no remote copies, remote signals or barrier semaphores. Data moves between devices by JAX's collectives and lax.ppermute only.
A program may use at most 128 MiB of HBM per device.

```python
import math
import jax
import jax.numpy as jnp
import numpy as np
from jax import lax

D = 512
HEADS = 8
FF = 2048
HEAD_DIM = 64
LENGTH = 2048
SEQS = 8


def shard_levels(own_key, dims, cuts, least, top_value):
    def one(position, shards_of):
        draws = jax.random.uniform(jax.random.fold_in(jax.random.fold_in(own_key, 6), position), (shards_of,), jnp.float32, least / len(cuts), top_value / len(cuts))
        return jnp.repeat(jnp.exp(draws), dims[position] // shards_of).reshape((-1,) + (1,) * (len(dims) - position - 1))

    loudness = one(*cuts[0])
    for cut in cuts[1:]:
        loudness = loudness * one(*cut)
    return loudness


def profile(count, total, bound, skew):
    loads = [(1 << 20) // math.isqrt(rank ** skew) + 1 for rank in range(2, count + 1)]
    rest, counts = total - bound - (count - 1), [1] * (count - 1)
    while rest > 0:
        candidates = [i for i in range(count - 1) if counts[i] < bound]
        pool, budget = sum([loads[i] for i in candidates]), rest
        for i in candidates:
            addition = min(bound - counts[i], max(1, budget * loads[i] // pool), rest)
            counts[i] = counts[i] + addition
            rest = rest - addition
    return np.array([bound] + counts)


def uneven_parts(stream_key, count, total, bound, slope):
    if count == 2:
        one = jax.random.randint(stream_key, (), max(1, total - bound), min(bound, total - 1) + 1)
        return jnp.stack([one, total - one])
    sizes = jnp.asarray(profile(count, total, bound, slope), jnp.int32)
    couples = (count - 1) // 2
    donor, taker = sizes[1:1 + 2 * couples:2], sizes[2:2 + 2 * couples:2]
    room = jnp.minimum(donor - 1, bound - taker)
    passed = jax.random.randint(jax.random.fold_in(stream_key, 1), (couples,), 0, 1 << 20) % (room + 1)
    sizes = sizes.at[1:1 + 2 * couples:2].set(donor - passed).at[2:2 + 2 * couples:2].set(taker + passed)
    return sizes[jax.random.permutation(jax.random.fold_in(stream_key, 2), count)]


def gaussian(stream_key, shape, width, limit, cuts=(), kind=jnp.bfloat16):
    values = width * jax.random.normal(stream_key, shape, jnp.float32)
    if cuts:
        values = values * shard_levels(stream_key, shape, cuts, -0.22, 0.18)
    return jnp.clip(values, -limit, limit).astype(kind)


def setup_inputs(seed: int = 0) -> dict:
    seeds = jax.random.split(jax.random.key(seed), 14)
    return {
        "tokens": gaussian(seeds[0], (LENGTH, SEQS, D), 1.0, 6.0, ((0, 8), (1, 4))),
        "segments": jax.vmap(lambda own: jnp.searchsorted(jnp.cumsum(uneven_parts(own, max(4, LENGTH // 256), LENGTH, LENGTH // 2, 2)), jnp.arange(LENGTH), side="right"))(jax.random.split(seeds[1], SEQS)).reshape((SEQS, LENGTH)).astype(jnp.int32),
        "scales": jnp.clip(1.0 + 0.18 * jax.random.normal(seeds[2], (D,), jnp.float32), 0.1, 1.9),
        "shifts": gaussian(seeds[3], (D,), 0.5, 3.0, (), jnp.float32),
        "project": gaussian(seeds[4], (D, 3, D), D ** -0.5, 0.25, ((2, 4),)),
        "combine": gaussian(seeds[5], (D, D), (D // 8) ** -0.5, 0.75, ((0, 4),)),
        "stretch": jnp.clip(1.0 + 0.18 * jax.random.normal(seeds[6], (D,), jnp.float32), 0.1, 1.9),
        "offset": gaussian(seeds[7], (D,), 0.5, 3.0, (), jnp.float32),
        "expand": gaussian(seeds[8], (D, FF), D ** -0.5, 0.25, ((1, 4),)),
        "boosts": gaussian(seeds[9], (FF,), 0.5, 3.0, ((0, 4),), jnp.float32),
        "shrink": gaussian(seeds[10], (FF, D), FF ** -0.5, 0.125, ((0, 4),)),
        "biases": gaussian(seeds[11], (D,), 0.5, 3.0, (), jnp.float32),
        "cotangent": gaussian(seeds[12], (LENGTH, SEQS, D), 1.0, 6.0, ((0, 8), (1, 4))),
    }


EPSILON = 1e-05
NEGATIVE = -1e+30
TOP_PRECISION = lax.Precision.HIGHEST

@jax.custom_vjp
def low(v):
    return lax.optimization_barrier(v.astype(jnp.bfloat16)).astype(jnp.float32)

@jax.custom_vjp
def lower_gradient(v):
    return v

def low_keep(v):
    return (low(v), None)

def low_pass(kept, grad):
    return (grad,)

def back_keep(v):
    return (v, None)

def back_low(kept, grad):
    return (low(grad),)
low.defvjp(low_keep, low_pass)
lower_gradient.defvjp(back_keep, back_low)

def normalize(values, gain_values, shift_values):
    center = values - lax.optimization_barrier(jnp.mean(values, axis=-1, keepdims=True))
    inverse = lax.rsqrt(lax.optimization_barrier(jnp.mean(center * center, axis=-1, keepdims=True)) + EPSILON)
    return center * inverse * gain_values + shift_values

def attend_sequence(operands):
    queries, keys_all, values_all, seg_row = operands
    row_total = queries.shape[0]
    block_rows = min(512, row_total)

    def one_block(pieces):
        query_block, query_segs = pieces
        scores = jnp.einsum('qhe,khe->hqk', query_block, keys_all, precision=TOP_PRECISION) * HEAD_DIM ** (-0.5)
        scores = lower_gradient(scores)
        matches = (query_segs[:, None] == seg_row[None, :])[None]
        scores = jnp.where(matches, scores, NEGATIVE)
        row_top = lax.optimization_barrier(jnp.max(scores, axis=-1, keepdims=True))
        weights = jnp.exp(scores - row_top)
        weights = low(weights / lax.optimization_barrier(jnp.sum(weights, axis=-1, keepdims=True)))
        return jnp.einsum('hqk,khe->qhe', weights, values_all, precision=TOP_PRECISION)
    stacked = (queries.reshape(row_total // block_rows, block_rows, HEADS, HEAD_DIM), seg_row.reshape(row_total // block_rows, block_rows))
    outputs = lax.map(jax.checkpoint(one_block), stacked)
    return outputs.reshape(row_total, HEADS, HEAD_DIM)

def forward(tokens, scales, shifts, project, combine, stretch, offset, expand, boosts, shrink, biases, segments):
    length_rows, seq_total, model_width = tokens.shape
    normed = low(normalize(tokens, scales, shifts))
    mixed = lower_gradient(low(jnp.einsum('lsd,dcf->lscf', normed, project, precision=TOP_PRECISION)))
    split = jnp.transpose(mixed.reshape(length_rows, seq_total, 3, HEADS, HEAD_DIM), (2, 1, 0, 3, 4))
    attended_output = lax.map(attend_sequence, (split[0], split[1], split[2], segments))
    attended_output = jnp.transpose(attended_output, (1, 0, 2, 3)).reshape(length_rows, seq_total, model_width)
    attended_output = lower_gradient(low(attended_output))
    joined_rows = lower_gradient(jnp.einsum('hju,uv->hjv', attended_output, combine, precision=TOP_PRECISION))
    middle_hidden = tokens + joined_rows
    second_projection = low(normalize(middle_hidden, stretch, offset))
    before_norm = lower_gradient(jnp.einsum('ypt,ta->ypa', second_projection, expand, precision=TOP_PRECISION) + boosts)
    active_values = low(jax.nn.gelu(before_norm, approximate=False))
    return middle_hidden + jnp.einsum('hju,uv->hjv', active_values, shrink, precision=TOP_PRECISION) + biases

def reference(tokens, segments, scales, shifts, project, combine, stretch, offset, expand, boosts, shrink, biases, cotangent):
    params = [array_value.astype(jnp.float32) for array_value in (tokens, scales, shifts, project, combine, stretch, offset, expand, boosts, shrink, biases)]

    def closed(tokens_f, scales_f, shifts_f, project_f, combine_f, stretch_f, offset_f, expand_f, boosts_f, shrink_f, biases_f):
        return forward(tokens_f, scales_f, shifts_f, project_f, combine_f, stretch_f, offset_f, expand_f, boosts_f, shrink_f, biases_f, segments)
    output_f, pullback = jax.vjp(closed, *params)
    grads = pullback(cotangent.astype(jnp.float32))
    return (output_f.astype(jnp.bfloat16), grads[0], grads[1], grads[2], grads[3], grads[4], grads[5], grads[6], grads[7], grads[8], grads[9], grads[10])
```

```python
import functools

import jax
import jax.numpy as jnp
from jax import lax
from jax.experimental import pallas as pl
from jax.experimental.pallas import tpu as pltpu
from jax.sharding import PartitionSpec as P

HEAD_DIM = 64
EPSILON = 1e-05
NEGATIVE = -1e30
ROOT_HALF = 0.7071067811865476
INV_ROOT_TAU = 0.3989422804014327
GROUP = ("ctx", "tensor")
SMALL_ROWS = 32
EXTRA_ROWS = 16


F32 = jnp.float32
BF16 = jnp.bfloat16


def dot(a, b, dims):
    return lax.dot_general(a, b, (dims, ((), ())), preferred_element_type=F32)


NN = ((1,), (0,))
NT = ((1,), (1,))
TN = ((0,), (0,))


def bits_of(count):
    return count.bit_length() - 1


def swap(values, axes, size, bit):
    pairs = [(i, i ^ (1 << bit)) for i in range(size)]
    return lax.ppermute(values, axes, pairs)


def reduce_halves(values, axis_name, size, dim):
    index = lax.axis_index(axis_name)
    for bit in range(bits_of(size)):
        half = values.shape[dim] // 2
        mine = (index >> bit) & 1
        kept = lax.dynamic_slice_in_dim(values, mine * half, half, dim)
        sent = lax.dynamic_slice_in_dim(values, (1 - mine) * half, half, dim)
        got = swap(sent, axis_name, size, bit)
        values = (kept.astype(F32) + got.astype(F32)).astype(BF16)
    return values


def gather_halves(values, axis_name, size, dim):
    index = lax.axis_index(axis_name)
    for bit in reversed(range(bits_of(size))):
        mine = (index >> bit) & 1
        got = swap(values, axis_name, size, bit)
        low = jnp.where(mine == 0, values, got)
        high = jnp.where(mine == 0, got, values)
        values = jnp.concatenate([low, high], axis=dim)
    return values


def exchange(blocks, size, order):
    count = bits_of(len(blocks))
    blocks = list(blocks)
    for bit in order:
        picks = [m for m in range(1 << count) if (m >> bit) & 1]
        got = swap(jnp.stack([blocks[m] for m in picks]), GROUP, size, bit)
        for n, m in enumerate(picks):
            blocks[m] = got[n]
    return blocks


def forward_kernel(order, owned, count_ref, list_ref, *refs):
    blocks = len(order)
    parts = refs[: len(refs) - 11]
    (weight_ref, scale_ref, shift_ref, rows_ref, cols_ref) = refs[len(parts) : len(parts) + 5]
    (mixed_ref, out_ref, wide_ref, log_ref) = refs[len(parts) + 5 : len(parts) + 9]
    keys_ref, score_ref = refs[len(parts) + 9 :]
    size = rows_ref.shape[2]
    spot = 0
    for part in parts:
        for piece in range(part.shape[0] // size):
            m = order[spot]
            spot += 1
            hat = part[piece * size : (piece + 1) * size, :].astype(F32)
            normed = (hat * scale_ref[...] + shift_ref[...]).astype(BF16)
            mixed = dot(weight_ref[...], normed, NT).astype(BF16)
            mixed_ref[m, :HEAD_DIM, :] = mixed[:HEAD_DIM] * BF16(HEAD_DIM ** (-0.5))
            mixed_ref[m, HEAD_DIM:, :] = mixed[HEAD_DIM:]
            keys_ref[m] = mixed[HEAD_DIM : 2 * HEAD_DIM].astype(F32).T.astype(BF16)

    def one_block(i, unused):
        total = count_ref[i]
        query = mixed_ref[i, :HEAD_DIM, :]
        row_segs = rows_ref[i]

        def score(n, top):
            j = list_ref[i * blocks + n]
            values = dot(keys_ref[j], query, NN)
            same = jnp.tile(cols_ref[j], (1, size // 128)) == row_segs
            values = jnp.where(same, values, NEGATIVE)
            score_ref[n] = values
            return jnp.maximum(top, jnp.max(values.reshape(size // 8, 8, size), axis=0))

        top = lax.fori_loop(0, total, score, jnp.full((8, size), NEGATIVE, F32))
        top = jnp.max(top, axis=0, keepdims=True)

        def weigh(n, running):
            sums, held = running
            j = list_ref[i * blocks + n]
            weights = jnp.exp(score_ref[n] - top)
            sums = sums + jnp.sum(weights.reshape(size // 8, 8, size), axis=0)
            held = held + dot(mixed_ref[j, 2 * HEAD_DIM :, :], weights.astype(BF16), NN)
            return (sums, held)

        sums, held = lax.fori_loop(
            0, total, weigh, (jnp.zeros((8, size), F32), jnp.zeros((HEAD_DIM, size), F32))
        )
        sums = jnp.sum(sums, axis=0, keepdims=True)
        result = held / sums
        wide_ref[i] = result
        out_ref[i] = result.astype(BF16)
        log_ref[i] = top + jnp.log(sums)
        return unused

    lax.fori_loop(0, owned, one_block, 0)


def attend(parts, order, owned, weight, scales, shifts, rows, cols, counts, lists):
    blocks = len(order)
    size = rows.shape[2]
    vmem = pl.BlockSpec(memory_space=pltpu.VMEM)
    smem = pl.BlockSpec(memory_space=pltpu.SMEM)
    return pl.pallas_call(
        functools.partial(forward_kernel, tuple(order), owned),
        name="attend_forward",
        in_specs=[smem, smem] + [vmem] * (len(parts) + 5),
        out_specs=[vmem] * 4,
        out_shape=[
            jax.ShapeDtypeStruct((blocks, 3 * HEAD_DIM, size), BF16),
            jax.ShapeDtypeStruct((owned, HEAD_DIM, size), BF16),
            jax.ShapeDtypeStruct((owned, HEAD_DIM, size), F32),
            jax.ShapeDtypeStruct((owned, 1, size), F32),
        ],
        scratch_shapes=[
            pltpu.VMEM((blocks, size, HEAD_DIM), BF16),
            pltpu.VMEM((blocks, size, size), F32),
        ],
        cost_estimate=pl.CostEstimate(
            flops=owned * blocks * size * size * 256 * 4,
            transcendentals=owned * blocks * size * size,
            bytes_accessed=blocks * size * 2048,
        ),
    )(counts, lists, *parts, weight, scales, shifts, rows, cols)


def backward_kernel(order, owned, count_ref, list_ref, *refs):
    blocks = len(order)
    parts = refs[: len(refs) - 16]
    (weight_ref, rows_ref, cols_ref, mixed_ref, grad_ref, wide_ref, log_ref) = refs[
        len(parts) : len(parts) + 7
    ]
    normed_ref, outer_ref = refs[len(parts) + 7 : len(parts) + 9]
    (
        grads_ref,
        queries_ref,
        inner_ref,
        query_sum_ref,
        joint_ref,
        key_sum_ref,
        value_sum_ref,
    ) = refs[len(parts) + 9 :]
    size = rows_ref.shape[2]
    for i in range(owned):
        grad = grad_ref[i]
        grads_ref[i] = grad.astype(F32).T.astype(BF16)
        queries_ref[i] = mixed_ref[i, :HEAD_DIM, :].astype(F32).T.astype(BF16)
        inner_ref[i] = jnp.sum(grad.astype(F32) * wide_ref[i], axis=0, keepdims=True)
        query_sum_ref[i] = jnp.zeros((HEAD_DIM, size), F32)

    def one_block(j, unused):
        key_t = mixed_ref[j, HEAD_DIM : 2 * HEAD_DIM, :]
        keys = key_t.astype(F32).T.astype(BF16)
        values = mixed_ref[j, 2 * HEAD_DIM :, :].astype(F32).T.astype(BF16)
        col_segs = jnp.tile(cols_ref[j], (1, size // 128))
        key_sum_ref[...] = jnp.zeros_like(key_sum_ref)
        value_sum_ref[...] = jnp.zeros_like(value_sum_ref)

        def one_pair(n, unused_pair):
            i = list_ref[j * owned + n]
            scores = dot(keys, mixed_ref[i, :HEAD_DIM, :], NN)
            scores = jnp.where(col_segs == rows_ref[i], scores - log_ref[i], NEGATIVE)
            weights = jnp.exp(scores)
            prob_grad = dot(values, grad_ref[i], NN)
            score_grad = (weights * (prob_grad - inner_ref[i])).astype(BF16)
            value_sum_ref[...] += dot(weights.astype(BF16), grads_ref[i], NN)
            key_sum_ref[...] += dot(score_grad, queries_ref[i], NN)
            query_sum_ref[i] += dot(key_t, score_grad, NN)
            return unused_pair

        lax.fori_loop(0, count_ref[j], one_pair, 0)
        joint_ref[j, HEAD_DIM : 2 * HEAD_DIM, :] = key_sum_ref[...].T.astype(BF16)
        joint_ref[j, 2 * HEAD_DIM :, :] = value_sum_ref[...].T.astype(BF16)
        return unused

    lax.fori_loop(0, blocks, one_block, 0)
    outer_ref[...] = jnp.zeros_like(outer_ref)
    spot = 0
    for part in parts:
        for piece in range(part.shape[0] // size):
            m = order[spot]
            spot += 1
            if m < owned:
                joint_ref[m, :HEAD_DIM, :] = (query_sum_ref[m] * HEAD_DIM ** (-0.5)).astype(BF16)
            else:
                joint_ref[m, :HEAD_DIM, :] = jnp.zeros((HEAD_DIM, size), BF16)
            joint = joint_ref[m]
            normed_ref[m] = dot(joint, weight_ref[...], TN).astype(BF16)
            outer_ref[: 3 * HEAD_DIM, :] += dot(
                joint, part[piece * size : (piece + 1) * size, :], NN
            )
            total = dot(jnp.ones((8, size), BF16), joint, NT)
            outer_ref[3 * HEAD_DIM : 3 * HEAD_DIM + 8, : 3 * HEAD_DIM] += total


def attend_back(parts, order, owned, weight, rows, cols, counts, lists, mixed, grads, wide, logs):
    blocks = len(order)
    size = rows.shape[2]
    width = weight.shape[1]
    vmem = pl.BlockSpec(memory_space=pltpu.VMEM)
    smem = pl.BlockSpec(memory_space=pltpu.SMEM)
    return pl.pallas_call(
        functools.partial(backward_kernel, tuple(order), owned),
        name="attend_backward",
        in_specs=[smem, smem] + [vmem] * (len(parts) + 7),
        out_specs=[vmem] * 2,
        out_shape=[
            jax.ShapeDtypeStruct((blocks, size, width), BF16),
            jax.ShapeDtypeStruct((3 * HEAD_DIM + EXTRA_ROWS, width), F32),
        ],
        scratch_shapes=[
            pltpu.VMEM((owned, size, HEAD_DIM), BF16),
            pltpu.VMEM((owned, size, HEAD_DIM), BF16),
            pltpu.VMEM((owned, 1, size), F32),
            pltpu.VMEM((owned, HEAD_DIM, size), F32),
            pltpu.VMEM((blocks, 3 * HEAD_DIM, size), BF16),
            pltpu.VMEM((size, HEAD_DIM), F32),
            pltpu.VMEM((size, HEAD_DIM), F32),
        ],
        cost_estimate=pl.CostEstimate(
            flops=owned * blocks * size * size * 256 * 10,
            transcendentals=owned * blocks * size * size,
            bytes_accessed=blocks * size * 4096,
        ),
    )(counts, lists, *parts, weight, rows, cols, mixed, grads, wide, logs)


def erf_gelu(values):
    return 0.5 * values * (1.0 + lax.erf(values * ROOT_HALF))


def middle_kernel(
    att_ref,
    token_ref,
    up_ref,
    combine_ref,
    expand_ref,
    shrink_ref,
    boosts_ref,
    vector_ref,
    encoded_ref,
    middle_grad_ref,
    att_grad_ref,
    packed_ref,
    outer_s,
    middle_s,
    hat_s,
    second_s,
    inverse_s,
    out_s,
    grad_s,
):
    step = pl.program_id(0)
    steps = pl.num_programs(0)
    seqs, width, rows = att_ref.shape
    hidden = expand_ref.shape[2]
    stretch = vector_ref[0:1, :]
    offset = vector_ref[1:2, :]
    biases = vector_ref[2:3, :]

    @pl.when(step == 0)
    def start():
        for s in range(seqs):
            here = slice(s * rows, (s + 1) * rows)
            joined = dot(att_ref[s], combine_ref[...], TN)
            middle = token_ref[s].astype(F32) + joined
            center = middle - jnp.mean(middle, axis=-1, keepdims=True)
            inverse = lax.rsqrt(jnp.mean(center * center, axis=-1, keepdims=True) + EPSILON)
            hat = center * inverse
            middle_s[here, :] = middle
            hat_s[here, :] = hat
            inverse_s[here, :] = inverse
            second_s[here, :] = (hat * stretch + offset).astype(BF16)
        out_s[...] = jnp.zeros_like(out_s)
        grad_s[...] = jnp.zeros_like(grad_s)

    second = second_s[...]
    upstream = up_ref[...].reshape(seqs * rows, width)
    before = dot(second, expand_ref[0], NN) + boosts_ref[0]
    curve = 0.5 * (1.0 + lax.erf(before * ROOT_HALF))
    active = (before * curve).astype(BF16)
    slope = curve + before * INV_ROOT_TAU * jnp.exp(-0.5 * before * before)
    out_s[...] += dot(active, shrink_ref[0], NN)
    active_grad = dot(upstream, shrink_ref[0], NT)
    before_grad = active_grad * slope
    low_grad = before_grad.astype(BF16)
    packed_ref[0, :width, :] = dot(second, low_grad, TN).astype(BF16)
    packed_ref[0, width : width + hidden, :] = dot(active, upstream, TN).astype(BF16)
    grad_s[...] += dot(low_grad, expand_ref[0], NT)
    base = width + hidden + width // steps
    packed_ref[0, base:, :] = jnp.zeros((packed_ref.shape[1] - base, width), BF16)
    packed_ref[0, base : base + 1, :] = jnp.sum(
        low_grad.astype(F32), axis=0, keepdims=True
    ).astype(BF16)

    @pl.when(step == steps - 1)
    def finish():
        up_wide = upstream.astype(F32)
        second_grad = grad_s[...]
        hat = hat_s[...]
        encoded = middle_s[...] + out_s[...] + biases
        lift = second_grad * stretch
        inner = jnp.mean(lift * hat, axis=-1, keepdims=True)
        middle_grad = up_wide + inverse_s[...] * (
            lift - jnp.mean(lift, axis=-1, keepdims=True) - hat * inner
        )
        low = middle_grad.astype(BF16)
        outer_s[0:1, :] = jnp.sum(second_grad * hat, axis=0, keepdims=True)
        outer_s[1:2, :] = jnp.sum(second_grad, axis=0, keepdims=True)
        outer_s[2:3, :] = jnp.sum(up_wide, axis=0, keepdims=True)
        total = jnp.zeros((width, width), F32)
        for s in range(seqs):
            here = slice(s * rows, (s + 1) * rows)
            encoded_ref[s] = encoded[here].astype(BF16)
            middle_grad_ref[s] = middle_grad[here]
            att_grad_ref[s] = dot(combine_ref[...], low[here], NT).astype(BF16)
            total = total + dot(att_ref[s], low[here], NN)
        outer_s[8:, :] = total


def middle(att, tokens, cotangent, combine, expand, shrink, boosts, vectors):
    seqs, width, rows = att.shape
    steps, unused, hidden = expand.shape
    packed_rows = width + hidden + width // steps + SMALL_ROWS
    whole = lambda *shape: pl.BlockSpec(shape, lambda k: (0,) * len(shape))
    return pl.pallas_call(
        middle_kernel,
        name="middle",
        grid=(steps,),
        in_specs=[
            whole(seqs, width, rows),
            whole(seqs, rows, width),
            whole(seqs, rows, width),
            whole(width, width),
            pl.BlockSpec((1, width, hidden), lambda k: (k, 0, 0)),
            pl.BlockSpec((1, hidden, width), lambda k: (k, 0, 0)),
            pl.BlockSpec((1, 1, hidden), lambda k: (k, 0, 0)),
            whole(8, width),
        ],
        out_specs=[
            whole(seqs, rows, width),
            whole(seqs, rows, width),
            whole(seqs, width, rows),
            pl.BlockSpec((1, packed_rows, width), lambda k: (k, 0, 0)),
            whole(8 + width, width),
        ],
        out_shape=[
            jax.ShapeDtypeStruct((seqs, rows, width), BF16),
            jax.ShapeDtypeStruct((seqs, rows, width), F32),
            jax.ShapeDtypeStruct((seqs, width, rows), BF16),
            jax.ShapeDtypeStruct((steps, packed_rows, width), BF16),
            jax.ShapeDtypeStruct((8 + width, width), F32),
        ],
        scratch_shapes=[
            pltpu.VMEM((seqs * rows, width), F32),
            pltpu.VMEM((seqs * rows, width), F32),
            pltpu.VMEM((seqs * rows, width), BF16),
            pltpu.VMEM((seqs * rows, 1), F32),
            pltpu.VMEM((seqs * rows, width), F32),
            pltpu.VMEM((seqs * rows, width), F32),
        ],
        cost_estimate=pl.CostEstimate(
            flops=seqs * rows * width * hidden * steps * 14,
            transcendentals=seqs * rows * hidden * steps * 2,
            bytes_accessed=16 << 20,
        ),
    )(att, tokens, cotangent, combine, expand, shrink, boosts, vectors)


def shards(
    tokens,
    segments,
    scales,
    shifts,
    project,
    combine,
    stretch,
    offset,
    expand,
    boosts,
    shrink,
    biases,
    cotangent,
):
    rows, seqs, width = tokens.shape
    ctx, tensor, dp = (lax.axis_size(n) for n in ("ctx", "tensor", "dp"))
    size = ctx * tensor
    feature = project.shape[2]
    heads_here = feature // HEAD_DIM
    heads = heads_here * tensor
    owned = heads
    hidden = expand.shape[1]
    ctx_at, tensor_at = lax.axis_index("ctx"), lax.axis_index("tensor")
    me = ctx_at * tensor + tensor_at
    slot = ctx_at % heads_here
    t_bits = bits_of(tensor)
    g_bits = bits_of(size)
    h_bits = bits_of(heads)

    token_rows = jnp.transpose(tokens, (1, 0, 2))
    up_rows = jnp.transpose(cotangent, (1, 0, 2))
    inputs = token_rows.astype(F32)
    center = inputs - jnp.mean(inputs, axis=-1, keepdims=True)
    inverse = lax.rsqrt(jnp.mean(center * center, axis=-1, keepdims=True) + EPSILON)
    hat_one = center * inverse
    hat_low = hat_one.astype(BF16)

    parts_of, order = [], None
    for s in range(seqs):
        held, numbers = [hat_low[s]], [0]
        across = list(range(1, g_bits))
        if s % 2:
            across = across[::-1]
        for bit in across:
            got = [swap(piece, GROUP, size, bit) for piece in held]
            held = held + got
            numbers = numbers + [n | (1 << bit) for n in numbers]
        ranked = sorted(range(len(numbers)), key=lambda p: numbers[p])
        held = [held[p] for p in ranked]
        numbers = [numbers[p] for p in ranked]
        near = jnp.concatenate(held, axis=0)
        parts_of.append([near, swap(near, GROUP, size, 0)])
        order = numbers + [n | 1 for n in numbers]

    flipped = combine.reshape(heads_here, HEAD_DIM, width)
    if heads_here == 2:
        flipped = jnp.where(slot == 0, flipped, flipped[::-1])
    boost_rows = jnp.zeros((16, width), BF16)
    own = jnp.concatenate([expand, shrink, flipped.reshape(feature, width)], axis=0)
    own, unused = lax.optimization_barrier((own, parts_of[-1][0]))
    boost_own = boosts.reshape(1, hidden)
    stacks, boost_list = [own], [boost_own]
    for bit in reversed(range(t_bits)):
        perm = [(i, i ^ (1 << bit)) for i in range(tensor)]
        stacks = stacks + [lax.ppermute(v, "tensor", perm) for v in stacks]
        boost_list = boost_list + [lax.ppermute(v, "tensor", perm) for v in boost_list]
    t_order = [0]
    for bit in reversed(range(t_bits)):
        t_order = t_order + [n | (1 << bit) for n in t_order]
    place = [t_order.index(k) for k in range(tensor)]
    expand_all = jnp.stack([stacks[p][:width] for p in place])
    shrink_all = jnp.stack([stacks[p][width : width + hidden] for p in place])
    combine_all = jnp.concatenate(
        [
            stacks[p][width + hidden + h * HEAD_DIM : width + hidden + (h + 1) * HEAD_DIM]
            for h in range(heads_here)
            for p in place
        ]
    )
    boosts_all = jnp.stack([boost_list[p] for p in place])

    numbers = jnp.bitwise_xor(jnp.arange(size), me)
    seg_blocks = jnp.take(segments.reshape(seqs, size, rows), numbers, axis=1)
    first, last = seg_blocks[:, :, 0], seg_blocks[:, :, -1]
    meets = (first[:, :owned, None] <= last[:, None, :]) & (
        first[:, None, :] <= last[:, :owned, None]
    )
    row_segs = seg_blocks[:, :, None, :]
    col_segs = jnp.broadcast_to(seg_blocks[..., None], seg_blocks.shape + (128,))

    def lists(table):
        counts = jnp.sum(table.astype(jnp.int32), axis=-1)
        ranks = jnp.cumsum(table.astype(jnp.int32), axis=-1) - 1
        n = table.shape[-1]
        hits = (ranks[..., None, :] == jnp.arange(n)[:, None]) & table[..., None, :]
        found = jnp.sum(jnp.where(hits, jnp.arange(n), 0), axis=-1)
        return counts, found.reshape(found.shape[0], -1)

    counts, found = lists(meets)
    counts_back, found_back = lists(jnp.swapaxes(meets, 1, 2))

    weight = lax.dynamic_slice_in_dim(project, slot * HEAD_DIM, HEAD_DIM, 2)
    weight = jnp.transpose(weight.reshape(width, 3 * HEAD_DIM))
    scale_row, shift_row = scales.reshape(1, width), shifts.reshape(1, width)

    saved, arrived = [], []
    for s in range(seqs):
        mixed, att, wide, logs = attend(
            parts_of[s],
            order,
            owned,
            weight,
            scale_row,
            shift_row,
            row_segs[s],
            col_segs[s],
            counts[s],
            found[s],
        )
        saved.append((mixed, wide, logs))
        got = exchange([att[m] for m in range(owned)], size, range(h_bits))
        arrived.append(jnp.concatenate(got))
    att_all = jnp.stack(arrived)

    vectors = jnp.concatenate(
        [jnp.stack([stretch, offset, biases]), jnp.zeros((5, width), F32)], axis=0
    )
    encoded, middle_grad, att_grad, packed, outer = middle(
        att_all, token_rows, up_rows, combine_all, expand_all, shrink_all, boosts_all, vectors
    )

    joined = outer[8:].reshape(heads_here, tensor, HEAD_DIM, width)
    joined = jnp.transpose(joined, (1, 0, 2, 3)).reshape(tensor, feature, width).astype(BF16)
    base = width + hidden
    packed = lax.dynamic_update_slice(packed, joined, (0, base, 0))
    smalls = jnp.broadcast_to(outer[:3].astype(BF16), (tensor, 3, width))
    packed = lax.dynamic_update_slice(packed, smalls, (0, base + feature + 1, 0))

    back = []
    for s in range(seqs):
        blocks = att_grad[s].reshape(owned, HEAD_DIM, rows)
        got = exchange([blocks[m] for m in range(owned)], size, range(h_bits))
        back.append(jnp.stack(got))

    sums = [packed[k] for k in range(tensor)]
    for bit in range(t_bits):
        keep = [k for k in range(len(sums)) if not k & 1]
        send = [k for k in range(len(sums)) if k & 1]
        perm = [(i, i ^ (1 << bit)) for i in range(tensor)]
        got = lax.ppermute(jnp.stack([sums[k] for k in send]), "tensor", perm)
        sums = [
            (sums[k].astype(F32) + got[n].astype(F32)).astype(BF16) for n, k in enumerate(keep)
        ]
    own = sums[0]
    if heads_here == 2:
        piece = own[base : base + feature].reshape(2, HEAD_DIM, width)
        piece = jnp.where(slot == 0, piece, piece[::-1]).reshape(feature, width)
        own = lax.dynamic_update_slice(own, piece, (base, 0))
    own = reduce_halves(own, "ctx", ctx, 0)
    own = reduce_halves(own, "dp", dp, 1)
    own = gather_halves(own, "dp", dp, 1)
    own = gather_halves(own, "ctx", ctx, 0).astype(F32)
    delta_expand = own[:width]
    delta_shrink = own[width:base]
    delta_combine = own[base : base + feature]
    base = base + feature
    delta_boosts, delta_stretch, delta_offset, delta_biases = (own[base + n] for n in range(4))

    outer_sum, grads_in = None, []
    for s in range(seqs):
        mixed, wide, logs = saved[s]
        normed_grad, outer = attend_back(
            parts_of[s],
            order,
            owned,
            weight,
            row_segs[s],
            col_segs[s],
            counts_back[s],
            found_back[s],
            mixed,
            back[s],
            wide,
            logs,
        )
        outer_sum = outer if outer_sum is None else outer_sum + outer
        held = {m: normed_grad[m] for m in range(size)}
        bits = list(range(1, g_bits))
        if s % 2:
            bits = bits[::-1]
        for bit in [0] + bits:
            keep = [m for m in sorted(held) if not (m >> bit) & 1]
            send = [m | (1 << bit) for m in keep]
            got = swap(jnp.stack([held[m] for m in send]), GROUP, size, bit)
            held = {
                m: (held[m].astype(F32) + got[n].astype(F32)).astype(BF16)
                for n, m in enumerate(keep)
            }
        grads_in.append(held[0])

    normed_grad = jnp.stack(grads_in).astype(F32)
    lift = normed_grad * scales
    inner = jnp.mean(lift * hat_one, axis=-1, keepdims=True)
    delta_tokens = middle_grad + inverse * (
        lift - jnp.mean(lift, axis=-1, keepdims=True) - hat_one * inner
    )

    outer = outer_sum.astype(BF16)
    for bit in range(bits_of(heads_here), bits_of(ctx)):
        got = swap(outer, "ctx", ctx, bit)
        outer = (outer.astype(F32) + got.astype(F32)).astype(BF16)
    outer = reduce_halves(outer, "dp", dp, 1)
    outer = gather_halves(outer, "dp", dp, 1)
    wide = outer.astype(F32)
    features = 3 * HEAD_DIM
    hat_part, col_part = wide[:features], wide[features, :features].reshape(features, 1)
    weight_wide = weight.astype(F32)
    vector_sums = jnp.stack(
        [jnp.sum(weight_wide * hat_part, axis=0), jnp.sum(weight_wide * col_part, axis=0)]
    )
    for bit in range(h_bits):
        vector_sums = vector_sums + swap(vector_sums, GROUP, size, bit)
    delta_scales, delta_shifts = vector_sums[0], vector_sums[1]
    others = [outer]
    for bit in range(bits_of(heads_here)):
        others = others + [swap(v, "ctx", ctx, bit) for v in others]
    pieces = []
    for v in others:
        v = v.astype(F32)
        full = v[:features] * scale_row + v[features, :features].reshape(features, 1) * shift_row
        pieces.append(full.reshape(3, HEAD_DIM, width))
    if heads_here == 2:
        low = jnp.where(slot == 0, pieces[0], pieces[1])
        high = jnp.where(slot == 0, pieces[1], pieces[0])
        pieces = [low, high]
    delta_project = jnp.concatenate(pieces, axis=1)
    delta_project = jnp.transpose(delta_project, (2, 0, 1))

    return (
        jnp.transpose(encoded, (1, 0, 2)),
        jnp.transpose(delta_tokens, (1, 0, 2)),
        delta_scales,
        delta_shifts,
        delta_project,
        delta_combine,
        delta_stretch,
        delta_offset,
        delta_expand,
        delta_boosts,
        delta_shrink,
        delta_biases,
    )


def solution(mesh):
    placed = (
        P(("ctx", "tensor"), "dp", None),
        P("dp", None),
        P(),
        P(),
        P(None, None, "tensor"),
        P("tensor", None),
        P(),
        P(),
        P(None, "tensor"),
        P("tensor"),
        P("tensor", None),
        P(),
        P(("ctx", "tensor"), "dp", None),
    )
    return jax.shard_map(
        shards,
        mesh=mesh,
        in_specs=placed,
        out_specs=(
            P(("ctx", "tensor"), "dp", None),
            P(("ctx", "tensor"), "dp", None),
            P(),
            P(),
            P(None, None, "tensor"),
            P("tensor", None),
            P(),
            P(),
            P(None, "tensor"),
            P("tensor"),
            P("tensor", None),
            P(),
        ),
        check_vma=False,
    )
```

```python
import functools

import jax
import jax.numpy as jnp
from jax import lax
from jax.experimental import pallas as pl
from jax.experimental.pallas import tpu as pltpu
from jax.sharding import PartitionSpec as P

HEAD_DIM = 64
EPSILON = 1e-05
NEGATIVE = -1e30
ROOT_HALF = 0.7071067811865476
INV_ROOT_TAU = 0.3989422804014327
GROUP = ("ctx", "tensor")
SMALL_ROWS = 64
EXTRA_ROWS = 16


F32 = jnp.float32
BF16 = jnp.bfloat16


def dot(a, b, dims):
    return lax.dot_general(a, b, (dims, ((), ())), preferred_element_type=F32)


NN = ((1,), (0,))
NT = ((1,), (1,))
TN = ((0,), (0,))


def bits_of(count):
    return count.bit_length() - 1


def add_low(first, *others):
    total = first.astype(F32)
    for other in others:
        total = total + other.astype(F32)
    return total.astype(BF16)


def hop(values, axes, size, mask):
    return lax.ppermute(values, axes, [(i, i ^ mask) for i in range(size)])


def part(values, index, count, dim):
    length = values.shape[dim] // count
    return lax.dynamic_slice_in_dim(values, index * length, length, dim)


def scatter_direct(values, axis_name, size, dim):
    index = lax.axis_index(axis_name)
    got = [
        hop(part(values, index ^ mask, size, dim), axis_name, size, mask)
        for mask in range(1, size)
    ]
    return add_low(part(values, index, size, dim), *got)


def gather_direct(values, axis_name, size, dim):
    index = lax.axis_index(axis_name)
    pieces = [values] + [hop(values, axis_name, size, mask) for mask in range(1, size)]
    length = values.shape[dim]
    shape = values.shape[:dim] + (length * size,) + values.shape[dim + 1 :]
    whole = jnp.zeros(shape, values.dtype)
    for mask, piece in enumerate(pieces):
        whole = lax.dynamic_update_slice_in_dim(whole, piece, (index ^ mask) * length, dim)
    return whole


def trade_heads(blocks, heads, size, me):
    if size == heads:
        return lax.all_to_all(blocks, GROUP, 0, 0, tiled=True)
    own = me % heads
    numbers = jnp.bitwise_xor(jnp.arange(heads), own)
    relative = jnp.take(blocks, numbers, axis=0)
    got = [relative[0]] + [hop(relative[m], GROUP, size, m) for m in range(1, heads)]
    return jnp.take(jnp.stack(got), numbers, axis=0)


def split_refs(refs, *counts):
    groups, at = [], 0
    for count in counts:
        groups.append(refs[at : at + count])
        at += count
    return groups


def block_column(seg_ref, s, j, size):
    row = seg_ref[s : s + 1, pl.ds(pl.multiple_of(j * size, size), size)]
    return jnp.broadcast_to(row, (128, size)).T


def block_row(seg_ref, s, j, size):
    return seg_ref[s : s + 1, pl.ds(pl.multiple_of(j * size, size), size)]


def key_range(ends_ref, s, j, blocks, size):
    first, last = ends_ref[s, j * size], ends_ref[s, j * size + size - 1]

    def count(n, running):
        low, high = running
        low = low + (ends_ref[s, n * size + size - 1] < first).astype(jnp.int32)
        high = high + (ends_ref[s, n * size] <= last).astype(jnp.int32)
        return (low, high)

    return lax.fori_loop(0, blocks, count, (jnp.int32(0), jnp.int32(0)))


def forward_kernel(order, owned, s, chained, *refs):
    blocks = len(order)
    (place_ref, ends_ref), parts, inputs, rest = split_refs(
        refs, 2, blocks, 4, len(refs) - blocks - 6
    )
    weight_ref, scale_ref, shift_ref, seg_ref = inputs
    if chained:
        rest = rest[1:]
    mixed_ref, out_ref, wide_ref, log_ref, keys_ref, score_ref, cols_ref = rest
    size = parts[0].shape[0]
    me = place_ref[0]
    base = place_ref[1]
    for spot, piece_ref in enumerate(parts):
        j = me ^ order[spot]
        normed = (piece_ref[...].astype(F32) * scale_ref[...] + shift_ref[...]).astype(BF16)
        mixed = dot(weight_ref[...], normed, NT).astype(BF16)
        mixed_ref[j, :HEAD_DIM, :] = mixed[:HEAD_DIM] * BF16(HEAD_DIM ** (-0.5))
        mixed_ref[j, HEAD_DIM:, :] = mixed[HEAD_DIM:]
        keys_ref[j] = mixed[HEAD_DIM : 2 * HEAD_DIM].astype(F32).T.astype(BF16)
        cols_ref[j] = block_column(seg_ref, s, j, size)

    def one_block(i, unused):
        at = base + i
        low, high = key_range(ends_ref, s, at, blocks, size)
        query = mixed_ref[at, :HEAD_DIM, :]
        row_segs = block_row(seg_ref, s, at, size)

        def score(j, top):
            values = dot(keys_ref[j], query, NN)
            same = jnp.tile(cols_ref[j], (1, size // 128)) == row_segs
            values = jnp.where(same, values, NEGATIVE)
            score_ref[j] = values
            return jnp.maximum(top, jnp.max(values.reshape(size // 8, 8, size), axis=0))

        top = lax.fori_loop(low, high, score, jnp.full((8, size), NEGATIVE, F32))
        top = jnp.max(top, axis=0, keepdims=True)

        def weigh(j, running):
            sums, held = running
            weights = jnp.exp(score_ref[j] - top)
            sums = sums + jnp.sum(weights.reshape(size // 8, 8, size), axis=0)
            held = held + dot(mixed_ref[j, 2 * HEAD_DIM :, :], weights.astype(BF16), NN)
            return (sums, held)

        sums, held = lax.fori_loop(
            low, high, weigh, (jnp.zeros((8, size), F32), jnp.zeros((HEAD_DIM, size), F32))
        )
        sums = jnp.sum(sums, axis=0, keepdims=True)
        result = held / sums
        wide_ref[i] = result
        out_ref[i, 0] = result.astype(BF16)
        log_ref[i] = top + jnp.log(sums)
        return unused

    lax.fori_loop(0, owned, one_block, 0)


def attend(place, parts, order, owned, s, weight, scales, shifts, segments, chain):
    blocks = len(order)
    size = parts[0].shape[0]
    seqs = segments.shape[0]
    vmem = pl.BlockSpec(memory_space=pltpu.VMEM)
    smem = pl.BlockSpec(memory_space=pltpu.SMEM)
    chained = chain is not None
    operands = [place, segments, *parts, weight, scales, shifts, segments]
    in_specs = [smem, smem] + [vmem] * (blocks + 4)
    aliases = {}
    if chained:
        aliases = {len(operands): 1}
        operands.append(chain)
        in_specs.append(pl.BlockSpec(memory_space=pl.ANY))
    return pl.pallas_call(
        functools.partial(forward_kernel, tuple(order), owned, s, chained),
        name="attend_forward",
        grid=(1,),
        in_specs=in_specs,
        out_specs=[
            vmem,
            pl.BlockSpec((owned, 1, HEAD_DIM, size), lambda g: (0, s, 0, 0)),
            vmem,
            vmem,
        ],
        out_shape=[
            jax.ShapeDtypeStruct((blocks, 3 * HEAD_DIM, size), BF16),
            jax.ShapeDtypeStruct((owned, seqs, HEAD_DIM, size), BF16),
            jax.ShapeDtypeStruct((owned, HEAD_DIM, size), F32),
            jax.ShapeDtypeStruct((owned, 1, size), F32),
        ],
        scratch_shapes=[
            pltpu.VMEM((blocks, size, HEAD_DIM), BF16),
            pltpu.VMEM((blocks, size, size), F32),
            pltpu.VMEM((blocks, size, 128), jnp.int32),
        ],
        input_output_aliases=aliases,
        cost_estimate=pl.CostEstimate(
            flops=owned * blocks * size * size * 256 * 4,
            transcendentals=owned * blocks * size * size,
            bytes_accessed=blocks * size * 2048,
        ),
    )(*operands)


def backward_kernel(order, paths, owned, s, last, *refs):
    blocks = len(order)
    (place_ref, ends_ref), parts, inputs, rest = split_refs(
        refs, 2, blocks, 6, len(refs) - blocks - 8
    )
    weight_ref, seg_ref, mixed_ref, grad_ref, wide_ref, log_ref = inputs
    before_ref = None
    if last:
        before_ref, rest = rest[0], rest[1:]
    keep_ref, send_ref, outer_ref = rest[:3]
    (
        grads_ref,
        queries_ref,
        inner_ref,
        query_sum_ref,
        joint_ref,
        key_sum_ref,
        value_sum_ref,
        total_ref,
    ) = rest[3:]
    size = parts[0].shape[0]
    me = place_ref[0]
    base = place_ref[1]
    for i in range(owned):
        grad = grad_ref[i, 0]
        grads_ref[i] = grad.astype(F32).T.astype(BF16)
        queries_ref[i] = mixed_ref[base + i, :HEAD_DIM, :].astype(F32).T.astype(BF16)
        inner_ref[i] = jnp.sum(grad.astype(F32) * wide_ref[i], axis=0, keepdims=True)
        query_sum_ref[i] = jnp.zeros((HEAD_DIM, size), F32)

    def one_block(j, unused):
        key_t = mixed_ref[j, HEAD_DIM : 2 * HEAD_DIM, :]
        keys = key_t.astype(F32).T.astype(BF16)
        values = mixed_ref[j, 2 * HEAD_DIM :, :].astype(F32).T.astype(BF16)
        col_segs = jnp.tile(block_column(seg_ref, s, j, size), (1, size // 128))
        key_sum_ref[...] = jnp.zeros_like(key_sum_ref)
        value_sum_ref[...] = jnp.zeros_like(value_sum_ref)
        low, high = key_range(ends_ref, s, j, blocks, size)
        low = jnp.maximum(low - base, 0)
        high = jnp.minimum(high - base, owned)

        def one_pair(i, unused_pair):
            scores = dot(keys, mixed_ref[base + i, :HEAD_DIM, :], NN)
            same = col_segs == block_row(seg_ref, s, base + i, size)
            weights = jnp.exp(jnp.where(same, scores - log_ref[i], NEGATIVE))
            prob_grad = dot(values, grad_ref[i, 0], NN)
            score_grad = (weights * (prob_grad - inner_ref[i])).astype(BF16)
            value_sum_ref[...] += dot(weights.astype(BF16), grads_ref[i], NN)
            key_sum_ref[...] += dot(score_grad, queries_ref[i], NN)
            query_sum_ref[i] += dot(key_t, score_grad, NN)
            return unused_pair

        lax.fori_loop(low, high, one_pair, 0)
        joint_ref[j, :HEAD_DIM, :] = jnp.zeros((HEAD_DIM, size), BF16)
        joint_ref[j, HEAD_DIM : 2 * HEAD_DIM, :] = key_sum_ref[...].T.astype(BF16)
        joint_ref[j, 2 * HEAD_DIM :, :] = value_sum_ref[...].T.astype(BF16)
        return unused

    lax.fori_loop(0, blocks, one_block, 0)
    for i in range(owned):
        joint_ref[base + i, :HEAD_DIM, :] = (query_sum_ref[i] * HEAD_DIM ** (-0.5)).astype(BF16)
    features = 3 * HEAD_DIM
    total_ref[...] = before_ref[...] if last else jnp.zeros_like(total_ref)
    half = size // 2
    for spot, piece_ref in enumerate(parts):
        m = order[spot]
        joint = joint_ref[me ^ m]
        normed = dot(joint, weight_ref[...], TN).astype(BF16)
        target_ref = send_ref if m & 1 else keep_ref
        for path, ranks in enumerate(paths):
            target_ref[path, ranks.index(m & ~1)] = normed[path * half : (path + 1) * half]
        total_ref[:features, :] += dot(joint, piece_ref[...], NN)
        total_ref[features : features + 8, :features] += dot(
            jnp.ones((8, size), BF16), joint, NT
        )
    outer_ref[...] = total_ref[...].astype(outer_ref.dtype)


def attend_back(
    place, parts, order, paths, owned, s, weight, segments, mixed, grads, wide, logs, before
):
    blocks = len(order)
    size = parts[0].shape[0]
    width = weight.shape[1]
    last = before is not None
    vmem = pl.BlockSpec(memory_space=pltpu.VMEM)
    smem = pl.BlockSpec(memory_space=pltpu.SMEM)
    in_specs = [smem, smem] + [vmem] * (blocks + 3)
    in_specs.append(pl.BlockSpec((owned, 1, HEAD_DIM, size), lambda g: (0, s, 0, 0)))
    in_specs += [vmem, vmem]
    operands = [place, segments, *parts, weight, segments, mixed, grads, wide, logs]
    if last:
        operands.append(before)
        in_specs.append(vmem)
    rows = 3 * HEAD_DIM + EXTRA_ROWS
    halves = jax.ShapeDtypeStruct((2, blocks // 2, size // 2, width), BF16)
    return pl.pallas_call(
        functools.partial(backward_kernel, tuple(order), paths, owned, s, last),
        name="attend_backward",
        grid=(1,),
        in_specs=in_specs,
        out_specs=[vmem] * 3,
        out_shape=[
            halves,
            halves,
            jax.ShapeDtypeStruct((rows, width), BF16 if last else F32),
        ],
        scratch_shapes=[
            pltpu.VMEM((owned, size, HEAD_DIM), BF16),
            pltpu.VMEM((owned, size, HEAD_DIM), BF16),
            pltpu.VMEM((owned, 1, size), F32),
            pltpu.VMEM((owned, HEAD_DIM, size), F32),
            pltpu.VMEM((blocks, 3 * HEAD_DIM, size), BF16),
            pltpu.VMEM((size, HEAD_DIM), F32),
            pltpu.VMEM((size, HEAD_DIM), F32),
            pltpu.VMEM((rows, width), F32),
        ],
        cost_estimate=pl.CostEstimate(
            flops=owned * blocks * size * size * 256 * 10,
            transcendentals=owned * blocks * size * size,
            bytes_accessed=blocks * size * 4096,
        ),
    )(*operands)


def middle_kernel(tensor, hidden, *refs):
    (place_ref, att_ref, token_ref, up_ref, vector_ref), weights, outs, scratch = split_refs(
        refs, 5, tensor, 5, 5
    )
    encoded_ref, middle_grad_ref, att_grad_ref, keep_ref, send_ref = outs
    middle_s, hat_s, grad_s, combine_s, outer_s = scratch
    owned, seqs, head, rows = att_ref.shape
    width = token_ref.shape[2]
    here_t = place_ref[2]
    feature = width // tensor
    span = owned // tensor
    stretch = vector_ref[0:1, :]
    offset = vector_ref[1:2, :]
    biases = vector_ref[2:3, :]
    base = width + hidden
    for k in range(tensor):
        at = here_t ^ k
        for h in range(span):
            combine_s[pl.ds((h * tensor + at) * head, head), :] = weights[k][
                base + h * head : base + (h + 1) * head, :
            ]
    combine = combine_s[...]
    att = []
    for s in range(seqs):
        here = slice(s * rows, (s + 1) * rows)
        att.append(att_ref[:, s].reshape(owned * head, rows))
        joined = dot(att[s], combine, TN)
        middle_s[here, :] = token_ref[s].astype(F32) + joined
    middle = middle_s[...]
    center = middle - jnp.mean(middle, axis=-1, keepdims=True)
    inverse = lax.rsqrt(jnp.mean(center * center, axis=-1, keepdims=True) + EPSILON)
    hat = center * inverse
    hat_s[...] = hat
    second = (hat * stretch + offset).astype(BF16)
    upstream = up_ref[...].reshape(seqs * rows, width)
    grad_s[...] = jnp.zeros_like(grad_s)
    middle_s[...] += biases
    for k in range(tensor):
        weight_ref = weights[k]
        packed_ref = send_ref if k & 1 else keep_ref
        n = k // 2
        expand = weight_ref[:width, :]
        shrink = weight_ref[width:base, :]
        spot = base + feature
        boosts = weight_ref[spot : spot + 1, :].astype(F32) + weight_ref[
            spot + 1 : spot + 2, :
        ].astype(F32)
        before = dot(second, expand, NN) + boosts
        curve = 0.5 * (1.0 + lax.erf(before * ROOT_HALF))
        active = (before * curve).astype(BF16)
        slope = curve + before * INV_ROOT_TAU * jnp.exp(-0.5 * before * before)
        middle_s[...] += dot(active, shrink, NN)
        low_grad = (dot(upstream, shrink, NT) * slope).astype(BF16)
        packed_ref[n, :width, :] = dot(second, low_grad, TN).astype(BF16)
        packed_ref[n, width:base, :] = dot(active, upstream, TN).astype(BF16)
        grad_s[...] += dot(low_grad, expand, NT)
        packed_ref[n, spot:, :] = jnp.zeros((packed_ref.shape[1] - spot, width), BF16)
        packed_ref[n, spot : spot + 1, :] = jnp.sum(
            low_grad.astype(F32), axis=0, keepdims=True
        ).astype(BF16)
    up_wide = upstream.astype(F32)
    second_grad = grad_s[...]
    hat = hat_s[...]
    lift = second_grad * stretch
    inner = jnp.mean(lift * hat, axis=-1, keepdims=True)
    middle_grad = up_wide + inverse * (
        lift - jnp.mean(lift, axis=-1, keepdims=True) - hat * inner
    )
    low = middle_grad.astype(BF16)
    smalls = [
        jnp.sum(second_grad * hat, axis=0, keepdims=True).astype(BF16),
        jnp.sum(second_grad, axis=0, keepdims=True).astype(BF16),
        jnp.sum(up_wide, axis=0, keepdims=True).astype(BF16),
    ]
    total = None
    for s in range(seqs):
        here = slice(s * rows, (s + 1) * rows)
        encoded_ref[s] = middle_s[here, :].astype(BF16)
        middle_grad_ref[s] = middle_grad[here]
        grads = dot(combine, low[here], NT).astype(BF16)
        att_grad_ref[:, s] = grads.reshape(owned, head, rows)
        more = dot(att[s], low[here], NN)
        total = more if total is None else total + more
    outer_s[...] = total
    for k in range(tensor):
        at = here_t ^ k
        packed_ref = send_ref if k & 1 else keep_ref
        for h in range(span):
            packed_ref[k // 2, base + h * head : base + (h + 1) * head, :] = outer_s[
                pl.ds((h * tensor + at) * head, head), :
            ].astype(BF16)
        for n, small in enumerate(smalls):
            packed_ref[k // 2, base + feature + 1 + n : base + feature + 2 + n, :] = small


def middle(place, att, tokens, cotangent, vectors, weights, hidden):
    owned, seqs, head, rows = att.shape
    width = tokens.shape[2]
    tensor = len(weights)
    packed_rows = width + hidden + width // tensor + SMALL_ROWS
    vmem = pl.BlockSpec(memory_space=pltpu.VMEM)
    smem = pl.BlockSpec(memory_space=pltpu.SMEM)
    return pl.pallas_call(
        functools.partial(middle_kernel, tensor, hidden),
        name="middle",
        in_specs=[smem] + [vmem] * (4 + tensor),
        out_specs=[vmem] * 5,
        out_shape=[
            jax.ShapeDtypeStruct((seqs, rows, width), BF16),
            jax.ShapeDtypeStruct((seqs, rows, width), F32),
            jax.ShapeDtypeStruct((owned, seqs, head, rows), BF16),
            jax.ShapeDtypeStruct((tensor // 2, packed_rows, width), BF16),
            jax.ShapeDtypeStruct((tensor // 2, packed_rows, width), BF16),
        ],
        scratch_shapes=[
            pltpu.VMEM((seqs * rows, width), F32),
            pltpu.VMEM((seqs * rows, width), F32),
            pltpu.VMEM((seqs * rows, width), F32),
            pltpu.VMEM((width, width), BF16),
            pltpu.VMEM((width, width), F32),
        ],
        cost_estimate=pl.CostEstimate(
            flops=seqs * rows * width * hidden * tensor * 14,
            transcendentals=seqs * rows * hidden * tensor * 2,
            bytes_accessed=16 << 20,
        ),
    )(place, att, tokens, cotangent, vectors, *weights)


def shards(
    tokens,
    segments,
    scales,
    shifts,
    project,
    combine,
    stretch,
    offset,
    expand,
    boosts,
    shrink,
    biases,
    cotangent,
):
    rows, seqs, width = tokens.shape
    ctx, tensor, dp = (lax.axis_size(n) for n in ("ctx", "tensor", "dp"))
    size = ctx * tensor
    feature = project.shape[2]
    heads_here = feature // HEAD_DIM
    heads = heads_here * tensor
    hidden = expand.shape[1]
    ctx_at, tensor_at = lax.axis_index("ctx"), lax.axis_index("tensor")
    me = ctx_at * tensor + tensor_at
    slot = ctx_at % heads_here
    g_bits = bits_of(size)
    place = jnp.stack([me, me // heads * heads, tensor_at]).astype(jnp.int32)

    token_rows = jnp.transpose(tokens, (1, 0, 2))
    inputs = token_rows.astype(F32)
    center = inputs - jnp.mean(inputs, axis=-1, keepdims=True)
    inverse = lax.rsqrt(jnp.mean(center * center, axis=-1, keepdims=True) + EPSILON)
    hat_one = center * inverse
    hat_low = hat_one.astype(BF16)

    parts_of, order = [], None
    for s in range(seqs):
        with jax.named_scope(f"hat_{s}"):
            held = {0: hat_low[s]}
            across = list(range(1, g_bits))
            for bit in across if s % 2 == 0 else across[::-1]:
                for m in list(held):
                    held[m | (1 << bit)] = hop(held[m], GROUP, size, 1 << bit)
            for m in list(held):
                held[m | 1] = hop(held[m], GROUP, size, 1)
            order = sorted(held)
            parts_of.append([held[m] for m in order])

    boost_high = boosts.astype(BF16)
    boost_low = (boosts - boost_high.astype(F32)).astype(BF16)
    boost_rows = jnp.concatenate(
        [boost_high[None], boost_low[None], jnp.zeros((14, hidden), BF16)], axis=0
    )
    own = jnp.concatenate([expand, shrink, combine, boost_rows], axis=0)
    own, unused = lax.optimization_barrier((own, parts_of[-1][-2]))
    with jax.named_scope("weights"):
        stack = {0: own}
        for bit in reversed(range(bits_of(tensor))):
            for k in list(stack):
                stack[k | (1 << bit)] = hop(stack[k], "tensor", tensor, 1 << bit)
        weights = [stack[k] for k in range(tensor)]

    weight = lax.dynamic_slice_in_dim(project, slot * HEAD_DIM, HEAD_DIM, 2)
    weight = jnp.transpose(weight.reshape(width, 3 * HEAD_DIM))
    scale_row, shift_row = scales.reshape(1, width), shifts.reshape(1, width)

    saved, att = [], None
    for s in range(seqs):
        with jax.named_scope(f"ahead_{s}"):
            mixed, att, wide, logs = attend(
                place,
                parts_of[s],
                order,
                heads,
                s,
                weight,
                scale_row,
                shift_row,
                segments,
                att,
            )
        saved.append((mixed, wide, logs))
    att = trade_heads(att, heads, size, me)

    vectors = jnp.concatenate(
        [jnp.stack([stretch, offset, biases]), jnp.zeros((5, width), F32)], axis=0
    )
    up_rows = jnp.transpose(cotangent, (1, 0, 2))
    with jax.named_scope("mid"):
        encoded, middle_grad, att_grad, kept, sent = middle(
            place, att, token_rows, up_rows, vectors, weights, hidden
        )
    with jax.named_scope("sum_core"):
        got = hop(sent, "tensor", tensor, 1)
    att_grad = trade_heads(att_grad, heads, size, me)

    sums = add_low(kept, got)
    cut = sums.shape[1] // 2

    def over_tensor(values, name):
        for bit in range(1, bits_of(tensor)):
            with jax.named_scope(f"{name}_{bit}"):
                half = values.shape[0] // 2
                pairs = values.reshape(half, 2, *values.shape[1:])
                values = add_low(pairs[:, 0], hop(pairs[:, 1], "tensor", tensor, 1 << bit))
        return values[0]

    def over(values, axis_name, count, dim, name):
        with jax.named_scope(name):
            return scatter_direct(values, axis_name, count, dim)

    def spread(values, axis_name, count, dim, name):
        with jax.named_scope(name):
            return gather_direct(values, axis_name, count, dim)

    first, other = sums[:, :cut], sums[:, cut:]
    first = over_tensor(first, "sum_a1")
    other = over(other, "ctx", ctx, 1, "sum_b1")
    first = over(first, "dp", dp, 1, "sum_a2")
    other = over_tensor(other, "sum_b2")
    first = over(first, "ctx", ctx, 0, "sum_a3")
    other = over(other, "dp", dp, 1, "sum_b3")
    first = spread(first, "dp", dp, 1, "put_a1")
    other = spread(other, "ctx", ctx, 0, "put_b1")
    first = spread(first, "ctx", ctx, 0, "put_a2")
    other = spread(other, "dp", dp, 1, "put_b2")
    own = jnp.concatenate([first, other], axis=0).astype(F32)
    base = width + hidden
    delta_expand = own[:width]
    delta_shrink = own[width:base]
    delta_combine = own[base : base + feature]
    base = base + feature
    delta_boosts, delta_stretch, delta_offset, delta_biases = (own[base + n] for n in range(4))

    bits = list(range(1, g_bits))
    tracks = [bits, bits[::-1]]

    def ranked(track):
        return sorted(
            range(0, size, 2), key=lambda m: sum(((m >> b) & 1) << (g_bits - n) for n, b in enumerate(track))
        )

    paths = [ranked(track) for track in tracks]
    outer, grads_in = None, []
    for s in range(seqs):
        mixed, wide, logs = saved[s]
        with jax.named_scope(f"back_{s}"):
            keep, send, outer = attend_back(
                place,
                parts_of[s],
                order,
                paths,
                heads,
                s,
                weight,
                segments,
                mixed,
                att_grad,
                wide,
                logs,
                outer,
            )
        with jax.named_scope(f"rows_{s}"):
            held = add_low(keep, hop(send, GROUP, size, 1))
            ends = []
            for path, track in enumerate(tracks):
                values = held[path]
                for bit in track:
                    half = values.shape[0] // 2
                    values = add_low(values[:half], hop(values[half:], GROUP, size, 1 << bit))
                ends.append(values[0])
            grads_in.append(jnp.concatenate(ends, axis=0))

    normed_grad = jnp.stack(grads_in).astype(F32)
    lift = normed_grad * scales
    inner = jnp.mean(lift * hat_one, axis=-1, keepdims=True)
    delta_tokens = middle_grad + inverse * (
        lift - jnp.mean(lift, axis=-1, keepdims=True) - hat_one * inner
    )

    features = 3 * HEAD_DIM
    with jax.named_scope("outer"):
        for bit in range(bits_of(heads_here), bits_of(ctx)):
            outer = add_low(outer, hop(outer, "ctx", ctx, 1 << bit))
        outer_part = scatter_direct(outer, "dp", dp, 1)
        outer = gather_direct(outer_part, "dp", dp, 1)
        wide = outer.astype(F32)
        hat_part, col_part = wide[:features], wide[features, :features].reshape(features, 1)
        weight_wide = weight.astype(F32)
        sums = jnp.stack(
            [jnp.sum(weight_wide * hat_part, axis=0), jnp.sum(weight_wide * col_part, axis=0)]
        )
        for bit in range(bits_of(heads)):
            sums = sums + hop(sums, GROUP, size, 1 << bit)
        delta_scales, delta_shifts = sums[0], sums[1]
        others = [outer]
        for bit in range(bits_of(heads_here)):
            others = others + [hop(v, "ctx", ctx, 1 << bit) for v in others]
    pieces = []
    for v in others:
        v = v.astype(F32)
        full = v[:features] * scale_row + v[features, :features].reshape(features, 1) * shift_row
        pieces.append(full.reshape(3, HEAD_DIM, width))
    if heads_here == 2:
        low = jnp.where(slot == 0, pieces[0], pieces[1])
        high = jnp.where(slot == 0, pieces[1], pieces[0])
        pieces = [low, high]
    delta_project = jnp.concatenate(pieces, axis=1)
    delta_project = jnp.transpose(delta_project, (2, 0, 1))

    return (
        jnp.transpose(encoded, (1, 0, 2)),
        jnp.transpose(delta_tokens, (1, 0, 2)),
        delta_scales,
        delta_shifts,
        delta_project,
        delta_combine,
        delta_stretch,
        delta_offset,
        delta_expand,
        delta_boosts,
        delta_shrink,
        delta_biases,
    )


def solution(mesh):
    placed = (
        P(("ctx", "tensor"), "dp", None),
        P("dp", None),
        P(),
        P(),
        P(None, None, "tensor"),
        P("tensor", None),
        P(),
        P(),
        P(None, "tensor"),
        P("tensor"),
        P("tensor", None),
        P(),
        P(("ctx", "tensor"), "dp", None),
    )
    return jax.shard_map(
        shards,
        mesh=mesh,
        in_specs=placed,
        out_specs=(
            P(("ctx", "tensor"), "dp", None),
            P(("ctx", "tensor"), "dp", None),
            P(),
            P(),
            P(None, None, "tensor"),
            P("tensor", None),
            P(),
            P(),
            P(None, "tensor"),
            P("tensor"),
            P("tensor", None),
            P(),
        ),
        check_vma=False,
    )
```
